32 devices in a mesh: dp: 4 (over y, x), ctx: 8 (over z, core).
Axes of the slice: x: 2, y: 2, z: 4, core: 2. Of those that a mesh axis runs over, the one named last changes fastest.
Arguments:
- queries: bfloat16 [4096, 64, 128], P(('dp', 'ctx')), parts along dimension 0, may hold values from -4.5 to 4.5
- keys: bfloat16 [4096, 8, 128], P(('dp', 'ctx')), parts along dimension 0, may hold values from -4.5 to 4.5
- values: bfloat16 [4096, 8, 128], P(('dp', 'ctx')), parts along dimension 0, may hold values from -6 to 6
- out_grad: bfloat16 [4096, 64, 128], P(('dp', 'ctx')), parts along dimension 0, may hold values from -48 to 48
- rand_blocks: int32 [256, 16, 3], P(('dp', 'ctx')), parts along dimension 0, may hold values from 0 to 15, as said below
- global_blocks: int32 [8], P('dp'), parts along dimension 0, may hold values from 0 to 15, as said below
Outputs:
- output: bfloat16 [4096, 64, 128], P(('dp', 'ctx')), parts along dimension 0
- query_grad: bfloat16 [4096, 64, 128], P(('dp', 'ctx')), parts along dimension 0
- key_grad: bfloat16 [4096, 8, 128], P(('dp', 'ctx')), parts along dimension 0
- value_grad: bfloat16 [4096, 8, 128], P(('dp', 'ctx')), parts along dimension 0
The draws below stay inside these ranges and needn't reach their ends.
There are 4 independent parts, one for each index of `dp`. The reference program is written for one: setup_inputs(seed, part) draws one part's arguments, and reference() takes and returns one part's arrays. A program takes and returns all parts, laid end to end along the dimension named above; each array names one. Nothing has to cross between parts.
Inputs may be any that keep to these rules, and one draw needn't show every extreme that they name: `rand_blocks`: for each query head and query block, 3 different blocks, none of them the query block or a block beside it (modulo 16), none of them a global block. `global_blocks`: 2 different blocks.
All inputs are finite; a program needn't handle non-finite values.
Results may differ from the reference program's by a relative error of at most 0.011.
Values may be sent and summed in bfloat16 or wider, within the bound.
A program may use at most 192 MiB of HBM per device.

```python
import math
import jax
import jax.numpy as jnp
from jax import lax

H = 64
KVH = 8
DH = 128
BLK = 64
GLOB = 2
RAND = 3
LEN = 1024
NB = 16


def pick_globals(key):
    order = jax.random.permutation(jax.random.fold_in(key, 11), NB)
    return order[:GLOB].astype(jnp.int32)


def draw_global_blocks(key, part):
    return pick_globals(key)


def draw_rand_blocks(key, part):
    glob_ids = pick_globals(key)
    block_ids = jnp.arange(NB, dtype=jnp.int32)
    distance = (block_ids[None, :] - block_ids[:, None]) % NB
    banned = jnp.logical_or(distance <= 1, distance == NB - 1)
    is_global = jnp.any(block_ids[:, None] == glob_ids[None, :], axis=1)
    banned = jnp.logical_or(banned, is_global[None, :])
    noise = jax.random.randint(jax.random.fold_in(key, 17), (H, NB, NB), 0, 262144)
    ranked = noise * 4096 + block_ids[None, None, :]
    ranked = jnp.where(banned[None, :, :], -1 - block_ids[None, None, :], ranked)
    picked = lax.top_k(ranked, RAND)[1]
    return picked.astype(jnp.int32)


def draw_queries(key, part):
    query_vals = jnp.clip(jax.random.normal(jax.random.fold_in(key, 23), (LEN, H, DH), jnp.float32), -4.0, 4.0)
    return query_vals.astype(jnp.bfloat16)


def draw_keys(key, part):
    key_vals = jnp.clip(jax.random.normal(jax.random.fold_in(key, 31), (LEN, KVH, DH), jnp.float32), -4.0, 4.0)
    return key_vals.astype(jnp.bfloat16)


def block_levels(key, extent, split, smallest, largest):
    level = 1.0
    for position, blocks in split:
        draws = jax.random.uniform(jax.random.fold_in(jax.random.fold_in(key, 6), position), (blocks,), jnp.float32, smallest / len(split), largest / len(split))
        level = level * jnp.repeat(jnp.exp(draws), extent[position] // blocks).reshape((-1,) + (1,) * (len(extent) - 1 - position))
    return level


def scatter_about(rng, extent, spread, bound, pieces=(), kind=jnp.bfloat16):
    values = jax.random.normal(rng, extent, jnp.float32) * spread
    if len(pieces) > 0:
        values = block_levels(rng, extent, pieces, -0.22, 0.18) * values
    return jnp.clip(values, min=-bound, max=bound).astype(kind)


def setup_inputs(seed: int = 0, part: int = 0) -> dict:
    key_of = jax.random.split(jax.random.key(seed), 7)
    part_splits = jax.random.split(jax.random.fold_in(key_of[6], part), 7)
    return {
        "queries": draw_queries(jax.random.fold_in(jax.random.fold_in(key_of[6], part), 71), part),
        "keys": draw_keys(jax.random.fold_in(jax.random.fold_in(key_of[6], part), 71), part),
        "values": scatter_about(part_splits[2], (LEN, KVH, DH), 1.0, 6.0, ((0, 8),)),
        "out_grad": scatter_about(part_splits[3], (LEN, H, DH), 8.0, 48.0, ((0, 8),)),
        "rand_blocks": draw_rand_blocks(jax.random.fold_in(jax.random.fold_in(key_of[6], part), 71), part),
        "global_blocks": draw_global_blocks(jax.random.fold_in(jax.random.fold_in(key_of[6], part), 71), part),
    }


def block_table(rand_head, global_blocks, block_count):
    row_ids = jnp.arange(block_count, dtype=jnp.int32)
    window = jnp.stack([(row_ids + block_count - 1) % block_count, row_ids, (row_ids + 1) % block_count], axis=1)
    glob_cols = jnp.broadcast_to(global_blocks.astype(jnp.int32)[None, :], (block_count, global_blocks.shape[0]))
    key_table = jnp.concatenate([window, glob_cols, rand_head.astype(jnp.int32)], axis=1)
    slot_count = key_table.shape[1]
    repeated = key_table[:, :, None] == key_table[:, None, :]
    earlier = jnp.arange(slot_count)[None, :] < jnp.arange(slot_count)[:, None]
    usable = jnp.logical_not(jnp.any(jnp.logical_and(repeated, earlier[None, :, :]), axis=2))
    return (key_table, usable)

def group_size(block_count, block_rows):
    return math.gcd(block_count, max(1, 512 // block_rows))

def contract(form, left, right):
    return jnp.einsum(form, left.astype(jnp.float32), right.astype(jnp.float32))

def forward_head(global_blocks, operands):
    query_h, key_h, value_h, rand_head = operands
    length, head_width = query_h.shape
    block_count = length // BLK
    per_step = group_size(block_count, BLK)
    step_count = block_count // per_step
    key_table, usable = block_table(rand_head, global_blocks, block_count)
    factor = 1.0 / math.sqrt(head_width)
    key_blocks = key_h.reshape(block_count, BLK, head_width)
    value_blocks = value_h.reshape(block_count, BLK, head_width)
    packs = (query_h.reshape(step_count, per_step, BLK, head_width), key_table.reshape(step_count, per_step, -1), usable.reshape(step_count, per_step, -1))

    def one_group(group_pack):
        query_g, table_g, usable_g = group_pack
        key_g = key_blocks[table_g].reshape(per_step, -1, head_width)
        value_g = value_blocks[table_g].reshape(per_step, -1, head_width)
        scores = contract('abd,akd->abk', query_g, key_g) * factor
        live_cols = jnp.repeat(usable_g, BLK, axis=1)[:, None, :]
        scores = jnp.where(live_cols, scores, -jnp.inf)
        row_max = lax.optimization_barrier(jnp.max(scores, axis=2, keepdims=True))
        raw_weight = jnp.exp(scores - row_max)
        prob_rows = (raw_weight / lax.optimization_barrier(jnp.sum(raw_weight, axis=2, keepdims=True))).astype(jnp.bfloat16)
        result = contract('abk,akd->abd', prob_rows, value_g).astype(jnp.bfloat16)
        return (result, prob_rows)
    result, prob_rows = lax.map(one_group, packs)
    return (result.reshape(length, head_width), prob_rows)

def backward_head(global_blocks, operands):
    query_h, key_h, value_h, grad_h, out_h, prob_all, rand_head = operands
    length, head_width = query_h.shape
    block_count = length // BLK
    per_step = group_size(block_count, BLK)
    step_count = block_count // per_step
    key_table, usable = block_table(rand_head, global_blocks, block_count)
    factor = 1.0 / math.sqrt(head_width)
    key_blocks = key_h.reshape(block_count, BLK, head_width)
    value_blocks = value_h.reshape(block_count, BLK, head_width)
    delta_all = lax.optimization_barrier(jnp.sum(grad_h.astype(jnp.float32) * out_h.astype(jnp.float32), axis=1))
    packs = (query_h.reshape(step_count, per_step, BLK, head_width), grad_h.reshape(step_count, per_step, BLK, head_width), delta_all.reshape(step_count, per_step, BLK), prob_all, key_table.reshape(step_count, per_step, -1))

    def one_group(carry, group_pack):
        key_acc, value_acc = carry
        query_g, grad_g, delta_g, prob_g, table_g = group_pack
        key_g = key_blocks[table_g].reshape(per_step, -1, head_width)
        value_g = value_blocks[table_g].reshape(per_step, -1, head_width)
        value_part = contract('abk,abd->akd', prob_g, grad_g)
        dprob = contract('abd,akd->abk', grad_g, value_g)
        dscore = (prob_g.astype(jnp.float32) * (dprob - delta_g[:, :, None])).astype(jnp.bfloat16)
        query_grad = (contract('abk,akd->abd', dscore, key_g) * factor).astype(jnp.bfloat16)
        key_part = contract('abk,abd->akd', dscore, query_g) * factor
        flat_ids = table_g.reshape(-1)
        key_acc = key_acc.at[flat_ids].add(key_part.reshape(-1, BLK, head_width))
        value_acc = value_acc.at[flat_ids].add(value_part.reshape(-1, BLK, head_width))
        return ((key_acc, value_acc), query_grad)
    zeros_acc = jnp.zeros((block_count, BLK, head_width), jnp.float32)
    (key_acc, value_acc), query_grad = lax.scan(one_group, (zeros_acc, zeros_acc), packs)
    return (query_grad.reshape(length, head_width), key_acc.reshape(length, head_width).astype(jnp.bfloat16), value_acc.reshape(length, head_width).astype(jnp.bfloat16))

def reference(queries, keys, values, out_grad, rand_blocks, global_blocks):
    heads_per_kv = H // KVH
    keys_wide = jnp.repeat(keys, heads_per_kv, axis=1)
    values_wide = jnp.repeat(values, heads_per_kv, axis=1)

    def per_head(head_pack):
        query_h, key_h, value_h, grad_h, rand_head = head_pack
        out_h, prob_all = forward_head(global_blocks, (query_h, key_h, value_h, rand_head))
        grads = backward_head(global_blocks, (query_h, key_h, value_h, grad_h, out_h, prob_all, rand_head))
        return (out_h, grads[0], grads[1], grads[2])
    out_all, query_all, key_parts, value_parts = lax.map(per_head, (jnp.moveaxis(queries, 1, 0), jnp.moveaxis(keys_wide, 1, 0), jnp.moveaxis(values_wide, 1, 0), jnp.moveaxis(out_grad, 1, 0), rand_blocks))
    output = jnp.moveaxis(out_all, 0, 1)
    query_grad = jnp.moveaxis(query_all, 0, 1)
    key_sum = key_parts.reshape(KVH, heads_per_kv, LEN, DH).astype(jnp.float32).sum(axis=1).astype(jnp.bfloat16)
    value_sum = value_parts.reshape(KVH, heads_per_kv, LEN, DH).astype(jnp.float32).sum(axis=1).astype(jnp.bfloat16)
    return (output, query_grad, jnp.moveaxis(key_sum, 0, 1), jnp.moveaxis(value_sum, 0, 1))
```

```python
import functools
import math

import jax
import jax.numpy as jnp
from jax import lax
from jax.experimental import pallas as pl
from jax.experimental.pallas import tpu as pltpu
from jax.sharding import PartitionSpec as P

BLK = 64
NT = (((1,), (1,)), ((), ()))
NN = (((1,), (0,)), ((), ()))


def dot(left, right, dims=NN):
    return lax.dot_general(left, right, dims, preferred_element_type=jnp.float32)


def flat_rows(block):
    rows = block.shape[0] * block.shape[1]
    return block.astype(jnp.float32).reshape(rows, block.shape[2])


def for_chunks(count, step, init):
    return lax.fori_loop(0, count, step, init, unroll=count <= 4)


def attention(geometry, q_ref, g_ref, kv_ref, bias_ref, out_ref, dq_ref, dkv_ref, s_buf, e_buf, acc):
    chunk, row_tile = geometry
    shards, _, _, shard_tokens, width = kv_ref.shape
    length = shards * shard_tokens
    count = length // chunk
    tokens, group, _ = q_ref.shape
    rows = tokens * group
    tiles = rows // row_tile
    tile_tokens = row_tile // group
    factor = 1.0 / math.sqrt(width)
    to_log2 = factor * math.log2(math.e)
    per_chunk = chunk // shard_tokens

    def kv_chunk(which, c):
        return kv_ref[pl.ds(c * per_chunk, per_chunk), 0, which].reshape(chunk, width)

    for tile in range(tiles):
        t0 = tile * tile_tokens
        lanes = pl.ds(tile * row_tile, row_tile)
        q = flat_rows(q_ref[pl.ds(t0, tile_tokens)]).astype(jnp.bfloat16)
        g32 = flat_rows(g_ref[pl.ds(t0, tile_tokens)])

        def score_step(c, top):
            s = dot(kv_chunk(0, c), q, NT) * to_log2
            blocks = chunk // BLK
            bias = bias_ref[0, pl.ds(c * blocks, blocks), :, lanes]
            s = (s.reshape(blocks, BLK, row_tile) + bias).reshape(chunk, row_tile)
            s_buf[pl.ds(c * chunk, chunk)] = s
            return jnp.maximum(top, jnp.max(s, axis=0, keepdims=True))

        top = for_chunks(count, score_step, jnp.full((1, row_tile), -jnp.inf, jnp.float32))

        def weight_step(c, carry):
            total, out_t = carry
            e = jnp.exp2(s_buf[pl.ds(c * chunk, chunk)] - top)
            total = total + jnp.sum(e, axis=0, keepdims=True)
            e16 = e.astype(jnp.bfloat16)
            e_buf[pl.ds(c * chunk, chunk)] = e16
            out_t = out_t + dot(kv_chunk(1, c).T, e16)
            return total, out_t

        total, out_t = for_chunks(
            count,
            weight_step,
            (jnp.zeros((1, row_tile), jnp.float32), jnp.zeros((width, row_tile), jnp.float32)),
        )
        inverse = 1.0 / total
        out16 = (out_t * inverse).T.astype(jnp.bfloat16)
        out32 = out16.astype(jnp.float32)
        out_ref[pl.ds(t0, tile_tokens)] = out32.reshape(tile_tokens, group, width).astype(jnp.bfloat16)
        delta = jnp.sum((g32 * out32).T, axis=0, keepdims=True) * inverse
        g16 = (g32.T * inverse).T.astype(jnp.bfloat16)

        def grad_step(c, dq_t):
            at = pl.ds(c * chunk, chunk)
            e16 = e_buf[at]
            dp = dot(kv_chunk(1, c), g16, NT)
            ds = (e16.astype(jnp.float32) * (dp - delta)).astype(jnp.bfloat16)
            dk = dot(ds, q)
            dv = dot(e16, g16)
            if tile > 0:
                dk = dk + acc[0, at]
                dv = dv + acc[1, at]
            if tile < tiles - 1:
                acc[0, at] = dk
                acc[1, at] = dv
            else:
                shape = (per_chunk, shard_tokens, width)
                spot = pl.ds(c * per_chunk, per_chunk)
                dkv_ref[spot, 0, 0] = (dk * factor).astype(jnp.bfloat16).reshape(shape)
                dkv_ref[spot, 0, 1] = dv.astype(jnp.bfloat16).reshape(shape)
            return dq_t + dot(kv_chunk(0, c).T, ds)

        dq_t = for_chunks(count, grad_step, jnp.zeros((width, row_tile), jnp.float32))
        dq = (dq_t * factor).T.reshape(tile_tokens, group, width)
        dq_ref[pl.ds(t0, tile_tokens)] = dq.astype(jnp.bfloat16)


def local_attention(queries, out_grad, kv, bias):
    tokens, heads, width = queries.shape
    shards, kv_heads, _, shard_tokens, _ = kv.shape
    group = heads // kv_heads
    length = shards * shard_tokens
    rows = tokens * group
    chunk = math.gcd(length, 256)
    row_tile = rows
    while row_tile * length > (1 << 21) and row_tile > 128:
        row_tile //= 2
    acc_rows = length if row_tile < rows else 8
    blocks = length // BLK
    q_spec = pl.BlockSpec((tokens, group, width), lambda g: (0, g, 0))
    kv_spec = pl.BlockSpec((shards, 1, 2, shard_tokens, width), lambda g: (0, g, 0, 0, 0))
    return pl.pallas_call(
        functools.partial(attention, (chunk, row_tile)),
        grid=(kv_heads,),
        in_specs=[
            q_spec,
            q_spec,
            kv_spec,
            pl.BlockSpec((1, blocks, 1, rows), lambda g: (g, 0, 0, 0)),
        ],
        out_specs=[q_spec, q_spec, kv_spec],
        out_shape=[
            jax.ShapeDtypeStruct(queries.shape, jnp.bfloat16),
            jax.ShapeDtypeStruct(queries.shape, jnp.bfloat16),
            jax.ShapeDtypeStruct(kv.shape, jnp.bfloat16),
        ],
        scratch_shapes=[
            pltpu.VMEM((length, row_tile), jnp.float32),
            pltpu.VMEM((length, row_tile), jnp.bfloat16),
            pltpu.VMEM((2, acc_rows, width), jnp.float32),
        ],
        compiler_params=pltpu.CompilerParams(vmem_limit_bytes=60 * 1024 * 1024),
        name="attention",
    )(queries, out_grad, kv, bias)


def row_bias(rand_all, global_blocks, first, here, block_count, kv_heads):
    heads = rand_all.shape[0]
    group = heads // kv_heads
    mine = lax.dynamic_slice_in_dim(rand_all, first, here, axis=1)
    ids = first + jnp.arange(here, dtype=jnp.int32)
    key_ids = jnp.arange(block_count, dtype=jnp.int32)
    away = (key_ids[None, :] - ids[:, None] + block_count + 1) % block_count
    common = (away <= 2) | jnp.any(key_ids[None, :, None] == global_blocks[None, None, :], axis=2)
    chosen = jnp.any(mine[:, :, None, :] == key_ids[None, None, :, None], axis=3)
    live = chosen | common[None]
    bias = jnp.where(live, 0.0, -jnp.inf).astype(jnp.float32)
    bias = bias.reshape(kv_heads, group, here, block_count).transpose(0, 3, 2, 1)
    bias = jnp.broadcast_to(bias[:, :, :, None, :], (kv_heads, block_count, here, BLK, group))
    return bias.reshape(kv_heads, block_count, 1, here * BLK * group)


def body(queries, keys, values, out_grad, rand_blocks, global_blocks):
    tokens, kv_heads, width = keys.shape
    here = tokens // BLK
    block_count = rand_blocks.shape[1]
    me = lax.axis_index("ctx")
    kv_here = jnp.stack([keys.transpose(1, 0, 2), values.transpose(1, 0, 2)], axis=1)
    kv = lax.all_gather(kv_here, "ctx", axis=0)
    rand_all = lax.all_gather(rand_blocks, "ctx", axis=0, tiled=True)
    bias = row_bias(rand_all, global_blocks, me * here, here, block_count, kv_heads)
    output, query_grad, parts = local_attention(queries, out_grad, kv, bias)
    sums = lax.psum_scatter(parts, "ctx", scatter_dimension=0, tiled=False)
    grads = sums.transpose(1, 2, 0, 3)
    return output, query_grad, grads[0], grads[1]


def solution(mesh):
    split = P(("dp", "ctx"), None, None)
    return jax.shard_map(
        body,
        mesh=mesh,
        in_specs=(split, split, split, split, split, P("dp")),
        out_specs=(split, split, split, split),
        check_vma=False,
    )
```

```python
import functools
import math

import jax
import jax.numpy as jnp
from jax import lax
from jax.experimental import pallas as pl
from jax.experimental.pallas import tpu as pltpu
from jax.sharding import PartitionSpec as P

BLK = 64
NT = (((1,), (1,)), ((), ()))
NN = (((1,), (0,)), ((), ()))


def dot(left, right, dims=NN):
    return lax.dot_general(left, right, dims, preferred_element_type=jnp.float32)


def flat_rows(block):
    rows = block.shape[0] * block.shape[1]
    return block.astype(jnp.float32).reshape(rows, block.shape[2])


def for_chunks(count, step, init):
    return lax.fori_loop(0, count, step, init, unroll=count <= 4)


def attention(geometry, q_ref, g_ref, kv_ref, bias_ref, out_ref, dq_ref, dkv_ref, s_buf, e_buf, acc):
    chunk, row_tile = geometry
    shards, _, _, shard_tokens, width = kv_ref.shape
    length = shards * shard_tokens
    count = length // chunk
    tokens, group, _ = q_ref.shape
    rows = tokens * group
    tiles = rows // row_tile
    tile_tokens = row_tile // group
    factor = 1.0 / math.sqrt(width)
    to_log2 = factor * math.log2(math.e)
    per_chunk = chunk // shard_tokens

    def kv_chunk(which, c):
        return kv_ref[pl.ds(c * per_chunk, per_chunk), 0, which].reshape(chunk, width)

    for tile in range(tiles):
        t0 = tile * tile_tokens
        lanes = pl.ds(tile * row_tile, row_tile)
        q = flat_rows(q_ref[pl.ds(t0, tile_tokens)]).astype(jnp.bfloat16)
        g32 = flat_rows(g_ref[pl.ds(t0, tile_tokens)])

        def score_step(c, top):
            s = dot(kv_chunk(0, c), q, NT) * to_log2
            blocks = chunk // BLK
            bias = bias_ref[0, pl.ds(c * blocks, blocks), :, lanes]
            s = (s.reshape(blocks, BLK, row_tile) + bias).reshape(chunk, row_tile)
            s_buf[pl.ds(c * chunk, chunk)] = s
            return jnp.maximum(top, jnp.max(s, axis=0, keepdims=True))

        top = for_chunks(count, score_step, jnp.full((1, row_tile), -jnp.inf, jnp.float32))

        def weight_step(c, carry):
            total, out_t = carry
            e = jnp.exp2(s_buf[pl.ds(c * chunk, chunk)] - top)
            total = total + jnp.sum(e, axis=0, keepdims=True)
            e16 = e.astype(jnp.bfloat16)
            e_buf[pl.ds(c * chunk, chunk)] = e16
            out_t = out_t + dot(kv_chunk(1, c).T, e16)
            return total, out_t

        total, out_t = for_chunks(
            count,
            weight_step,
            (jnp.zeros((1, row_tile), jnp.float32), jnp.zeros((width, row_tile), jnp.float32)),
        )
        inverse = 1.0 / total
        out16 = (out_t * inverse).T.astype(jnp.bfloat16)
        out32 = out16.astype(jnp.float32)
        out_ref[pl.ds(t0, tile_tokens)] = out32.reshape(tile_tokens, group, width).astype(jnp.bfloat16)
        delta = jnp.sum((g32 * out32).T, axis=0, keepdims=True) * inverse
        g16 = (g32.T * inverse).T.astype(jnp.bfloat16)

        def grad_step(c, dq_t):
            at = pl.ds(c * chunk, chunk)
            e16 = e_buf[at]
            dp = dot(kv_chunk(1, c), g16, NT)
            ds = (e16.astype(jnp.float32) * (dp - delta)).astype(jnp.bfloat16)
            dk = dot(ds, q)
            dv = dot(e16, g16)
            if tile > 0:
                dk = dk + acc[0, at]
                dv = dv + acc[1, at]
            if tile < tiles - 1:
                acc[0, at] = dk
                acc[1, at] = dv
            else:
                shape = (per_chunk, shard_tokens, width)
                spot = pl.ds(c * per_chunk, per_chunk)
                dkv_ref[spot, 0, 0] = (dk * factor).astype(jnp.bfloat16).reshape(shape)
                dkv_ref[spot, 0, 1] = dv.astype(jnp.bfloat16).reshape(shape)
            return dq_t + dot(kv_chunk(0, c).T, ds)

        dq_t = for_chunks(count, grad_step, jnp.zeros((width, row_tile), jnp.float32))
        dq = (dq_t * factor).T.reshape(tile_tokens, group, width)
        dq_ref[pl.ds(t0, tile_tokens)] = dq.astype(jnp.bfloat16)


def local_attention(queries, out_grad, kv, bias):
    tokens, heads, width = queries.shape
    shards, kv_heads, _, shard_tokens, _ = kv.shape
    group = heads // kv_heads
    length = shards * shard_tokens
    rows = tokens * group
    chunk = math.gcd(length, 256)
    row_tile = rows
    while row_tile * length > (1 << 21) and row_tile > 128:
        row_tile //= 2
    acc_rows = length if row_tile < rows else 8
    blocks = length // BLK
    q_spec = pl.BlockSpec((tokens, group, width), lambda g: (0, g, 0))
    kv_spec = pl.BlockSpec((shards, 1, 2, shard_tokens, width), lambda g: (0, g, 0, 0, 0))
    return pl.pallas_call(
        functools.partial(attention, (chunk, row_tile)),
        grid=(kv_heads,),
        in_specs=[
            q_spec,
            q_spec,
            kv_spec,
            pl.BlockSpec((1, blocks, 1, rows), lambda g: (g, 0, 0, 0)),
        ],
        out_specs=[q_spec, q_spec, kv_spec],
        out_shape=[
            jax.ShapeDtypeStruct(queries.shape, jnp.bfloat16),
            jax.ShapeDtypeStruct(queries.shape, jnp.bfloat16),
            jax.ShapeDtypeStruct(kv.shape, jnp.bfloat16),
        ],
        scratch_shapes=[
            pltpu.VMEM((length, row_tile), jnp.float32),
            pltpu.VMEM((length, row_tile), jnp.bfloat16),
            pltpu.VMEM((2, acc_rows, width), jnp.float32),
        ],
        compiler_params=pltpu.CompilerParams(vmem_limit_bytes=60 * 1024 * 1024),
        name="attention",
    )(queries, out_grad, kv, bias)


def row_bias(rand_all, global_blocks, first, here, block_count, kv_heads):
    heads = rand_all.shape[0]
    group = heads // kv_heads
    mine = lax.dynamic_slice_in_dim(rand_all, first, here, axis=1)
    ids = first + jnp.arange(here, dtype=jnp.int32)
    key_ids = jnp.arange(block_count, dtype=jnp.int32)
    away = (key_ids[None, :] - ids[:, None] + block_count + 1) % block_count
    common = (away <= 2) | jnp.any(key_ids[None, :, None] == global_blocks[None, None, :], axis=2)
    chosen = jnp.any(mine[:, :, None, :] == key_ids[None, None, :, None], axis=3)
    live = chosen | common[None]
    bias = jnp.where(live, 0.0, -jnp.inf).astype(jnp.float32)
    bias = bias.reshape(kv_heads, group, here, block_count).transpose(0, 3, 2, 1)
    bias = jnp.broadcast_to(bias[:, :, :, None, :], (kv_heads, block_count, here, BLK, group))
    return bias.reshape(kv_heads, block_count, 1, here * BLK * group)


def fused_kernel(
    ids_in, kv_in, q_hbm, g_hbm, out_hbm, dq_hbm, grads_ref,
    q_buf, g_buf, o_buf, dq_buf, kv_buf, part_buf, sib_in, right_in, left_in, right_out, left_out,
    ids_buf, bias_buf, s_buf, e_buf,
    q_sem, g_sem, o_sem, dq_sem,
    ids_send, ids_recv, sib_send, sib_recv, fwd_send, fwd_recv, back_send, back_recv,
    pair_send, pair_recv, right_send, right_recv, left_send, left_recv,
):
    heads, _, chips, _, shard_tokens, width = kv_buf.shape
    shards = 2 * chips
    _, tokens, group, _ = q_buf.shape
    rows = tokens * group
    here = tokens // BLK
    block_count = shards * here
    half = BLK * group
    factor = 1.0 / math.sqrt(width)
    to_log2 = factor * math.log2(math.e)
    me = lax.axis_index("ctx")
    z, core = me // 2, me % 2
    pair = z * 2 + 1 - core
    ahead, behind = me + 2, me - 2
    last = chips - 1

    def send(source, target, send_sem, recv_sem, to):
        return pltpu.make_async_remote_copy(
            src_ref=source, dst_ref=target, send_sem=send_sem, recv_sem=recv_sem,
            device_id={"ctx": to}, device_id_type=pl.DeviceIdType.MESH,
        )

    def send_ids(k):
        to = lax.rem(me + k, shards)
        return send(ids_in.at[to], ids_buf.at[me], ids_send.at[k], ids_recv.at[me], to)

    def got_ids(k):
        origin = lax.rem(me + k, shards)
        return send(ids_in.at[origin], ids_buf.at[origin], ids_send.at[k], ids_recv.at[origin], origin)

    def kv_move(h, origin, lane, sems, to):
        spot = kv_buf.at[h, lane, origin]
        return send(spot, spot, sems[0].at[h, origin], sems[1].at[h, origin], to)

    sib_sems, fwd_sems, back_sems = (sib_send, sib_recv), (fwd_send, fwd_recv), (back_send, back_recv)

    def pair_move(h):
        return send(part_buf.at[h, 1 - core], sib_in.at[h], pair_send.at[h], pair_recv.at[h], pair)

    def right_move(h, zd):
        return send(right_out.at[h, zd], right_in.at[h, zd], right_send.at[h, zd], right_recv.at[h, zd], ahead)

    def left_move(h, zd):
        return send(left_out.at[h, zd], left_in.at[h, zd], left_send.at[h, zd], left_recv.at[h, zd], behind)

    def head_columns(ref, h):
        return ref.at[:, pl.ds(pl.multiple_of(h * group, group), group), :]

    def load_q(h):
        return pltpu.make_async_copy(head_columns(q_hbm, h), q_buf.at[h], q_sem.at[h])

    def load_g(h):
        return pltpu.make_async_copy(head_columns(g_hbm, h), g_buf.at[h], g_sem.at[h])

    def store_o(h):
        return pltpu.make_async_copy(o_buf.at[h], head_columns(out_hbm, h), o_sem.at[h])

    def store_dq(h):
        return pltpu.make_async_copy(dq_buf.at[h], head_columns(dq_hbm, h), dq_sem.at[h])

    def each_head(step):
        def run(h, carry):
            step(h)
            return carry
        lax.fori_loop(0, heads, run, 0)

    def start_loads(h):
        load_q(h).start()
        load_g(h).start()

    def place_own(h):
        kv_buf[h, core, z] = kv_in[h]

    each_head(start_loads)
    each_head(place_own)
    ids_buf[me] = ids_in[me]

    barrier = pltpu.get_barrier_semaphore()
    for k in range(1, shards):
        pl.semaphore_signal(
            barrier, inc=1, device_id={"ctx": lax.rem(me + k, shards)}, device_id_type=pl.DeviceIdType.MESH
        )
    pl.semaphore_wait(barrier, shards - 1)

    def forward_kv(h, origin, rightward, leftward):
        @pl.when(rightward)
        def _():
            kv_move(h, origin, core, fwd_sems, ahead).start()

        @pl.when(leftward)
        def _():
            kv_move(h, origin, core, back_sems, behind).start()

        kv_move(h, origin, core, sib_sems, pair).start()

    def both(h):
        return part_buf[h, core].astype(jnp.float32), sib_in[h].astype(jnp.float32)

    def combined(h, zd):
        return part_buf[h, core, zd].astype(jnp.float32) + sib_in[h, zd].astype(jnp.float32)

    def in_heads(h):
        return jnp.logical_and(h >= 0, h < heads)

    def reduce_right(h):
        for zd in range(1, chips):
            @pl.when(zd > z)
            def _(zd=zd):
                @pl.when(z == 0)
                def _():
                    right_out[h, zd] = combined(h, zd).astype(jnp.bfloat16)

                @pl.when(z > 0)
                def _():
                    right_move(h, zd).wait_recv()
                    total = combined(h, zd) + right_in[h, zd].astype(jnp.float32)
                    right_out[h, zd] = total.astype(jnp.bfloat16)

                right_move(h, zd).start()

    def reduce_left(h):
        for zd in range(chips - 1):
            @pl.when(zd < z)
            def _(zd=zd):
                @pl.when(z == last)
                def _():
                    left_out[h, zd] = combined(h, zd).astype(jnp.bfloat16)

                @pl.when(z < last)
                def _():
                    left_move(h, zd).wait_recv()
                    total = combined(h, zd) + left_in[h, zd].astype(jnp.float32)
                    left_out[h, zd] = total.astype(jnp.bfloat16)

                left_move(h, zd).start()

    def finish(h):
        @pl.when(z > 0)
        def _():
            right_move(h, z).wait_recv()

        @pl.when(z < last)
        def _():
            left_move(h, z).wait_recv()

        @pl.when(z == 0)
        def _():
            grads_ref[h] = (combined(h, z) + left_in[h, z].astype(jnp.float32)).astype(jnp.bfloat16)

        @pl.when(z == last)
        def _():
            grads_ref[h] = (combined(h, z) + right_in[h, z].astype(jnp.float32)).astype(jnp.bfloat16)

        @pl.when(jnp.logical_and(z > 0, z < last))
        def _():
            arrived = right_in[h, z].astype(jnp.float32) + left_in[h, z].astype(jnp.float32)
            grads_ref[h] = (combined(h, z) + arrived).astype(jnp.bfloat16)

    def compute(h):
        load_q(h).wait()
        load_g(h).wait()
        q = flat_rows(q_buf[h]).astype(jnp.bfloat16)
        g32 = flat_rows(g_buf[h])
        ids = ids_buf[h]
        key_ids = lax.broadcasted_iota(jnp.int32, (block_count, ids.shape[1]), 0)
        slots = (ids.shape[0] - 2) // here
        for b in range(here):
            away = key_ids - (me * here + b) + (block_count + 1)
            for _ in range(2):
                away = jnp.where(away >= block_count, away - block_count, away)
            live = (away <= 2) | (key_ids == ids[6:7]) | (key_ids == ids[7:8])
            for k in range(slots):
                live = live | (key_ids == ids[b * slots + k:b * slots + k + 1])
            bias = jnp.where(live, 0.0, -jnp.inf).astype(jnp.float32)
            reps = half // ids.shape[1]
            bias_buf[:, b * half:(b + 1) * half] = jnp.concatenate([bias] * reps, axis=1)

        chunk = 2 * shard_tokens
        spans = [(lane, zz) for lane in range(2) for zz in range(0, chips, 2)]

        def kv_chunk(which, span):
            return kv_buf[h, span[0], span[1]:span[1] + 2, which].reshape(chunk, width)

        top = None
        for c, span in enumerate(spans):
            s = dot(kv_chunk(0, span), q, NT) * to_log2
            pieces = []
            for j in range(2 * here):
                block = ((span[1] + j // here) * 2 + span[0]) * here + j % here
                pieces.append(s[j * BLK:(j + 1) * BLK] + bias_buf[block:block + 1])
            s = jnp.concatenate(pieces, axis=0)
            s_buf[c * chunk:(c + 1) * chunk] = s
            here_top = jnp.max(s, axis=0, keepdims=True)
            top = here_top if top is None else jnp.maximum(top, here_top)

        total = jnp.zeros((1, rows), jnp.float32)
        out_t = jnp.zeros((width, rows), jnp.float32)
        for c, span in enumerate(spans):
            e = jnp.exp2(s_buf[c * chunk:(c + 1) * chunk] - top)
            total = total + jnp.sum(e, axis=0, keepdims=True)
            e16 = e.astype(jnp.bfloat16)
            e_buf[c * chunk:(c + 1) * chunk] = e16
            out_t = out_t + dot(kv_chunk(1, span).T, e16)
        inverse = 1.0 / total
        out16 = (out_t * inverse).T.astype(jnp.bfloat16)
        out32 = out16.astype(jnp.float32)
        o_buf[h] = out32.reshape(tokens, group, width).astype(jnp.bfloat16)
        store_o(h).start()
        delta = jnp.sum((g32 * out32).T, axis=0, keepdims=True) * inverse
        g16 = (g32.T * inverse).T.astype(jnp.bfloat16)

        dq_t = jnp.zeros((width, rows), jnp.float32)
        for c, span in enumerate(spans):
            e16 = e_buf[c * chunk:(c + 1) * chunk]
            dp = dot(kv_chunk(1, span), g16, NT)
            ds = (e16.astype(jnp.float32) * (dp - delta)).astype(jnp.bfloat16)
            shape = (2, shard_tokens, width)
            dk = (dot(ds, q) * factor).astype(jnp.bfloat16)
            dv = dot(e16, g16).astype(jnp.bfloat16)
            part_buf[h, span[0], span[1]:span[1] + 2, 0] = dk.reshape(shape)
            part_buf[h, span[0], span[1]:span[1] + 2, 1] = dv.reshape(shape)
            dq_t = dq_t + dot(kv_chunk(0, span).T, ds)
        pair_move(h).start()
        dq = (dq_t * factor).T.reshape(tokens, group, width)
        dq_buf[h] = dq.astype(jnp.bfloat16)
        store_dq(h).start()

    lag = chips

    def slot(t, carry):
        for d in range(1, chips):
            h = t - d

            @pl.when(in_heads(h))
            def _(h=h, d=d):
                @pl.when(z - d >= 0)
                def _():
                    kv_move(h, z - d, core, fwd_sems, ahead).wait_recv()
                    forward_kv(h, z - d, z < last, z < 0)

                @pl.when(z + d <= last)
                def _():
                    kv_move(h, z + d, core, back_sems, behind).wait_recv()
                    forward_kv(h, z + d, z < 0, z > 0)

        @pl.when(t < heads)
        def _():
            forward_kv(t, z, z < last, z > 0)

        @pl.when(t == 0)
        def _():
            for k in range(1, shards):
                send_ids(k).start()

        e = t - lag - 1

        @pl.when(in_heads(e))
        def _():
            pair_move(e).wait_recv()

        @pl.when(jnp.logical_and(in_heads(e - z), z < last))
        def _():
            reduce_right(e - z)

        @pl.when(jnp.logical_and(in_heads(e - (last - z)), z > 0))
        def _():
            reduce_left(e - (last - z))

        f = e - jnp.maximum(z, last - z)

        @pl.when(in_heads(f))
        def _():
            finish(f)

        @pl.when(t == lag)
        def _():
            for k in range(1, shards):
                got_ids(k).wait_recv()

        @pl.when(in_heads(t - lag))
        def _():
            for origin in range(chips):
                kv_move(t - lag, origin, 1 - core, sib_sems, pair).wait_recv()
            compute(t - lag)

        return carry

    lax.fori_loop(0, heads + lag + chips, slot, 0)

    for k in range(1, shards):
        send_ids(k).wait_send()

    def drain(h):
        store_o(h).wait()
        store_dq(h).wait()
        pair_move(h).wait_send()
        for origin in range(chips):
            kv_move(h, origin, core, sib_sems, pair).wait_send()

            @pl.when(jnp.logical_and(origin <= z, z < last))
            def _(origin=origin):
                kv_move(h, origin, core, fwd_sems, ahead).wait_send()

            @pl.when(jnp.logical_and(origin >= z, z > 0))
            def _(origin=origin):
                kv_move(h, origin, core, back_sems, behind).wait_send()

            @pl.when(origin > z)
            def _(origin=origin):
                right_move(h, origin).wait_send()

            @pl.when(origin < z)
            def _(origin=origin):
                left_move(h, origin).wait_send()

    each_head(drain)


def fused(queries, out_grad, kv_here, ids):
    tokens, heads, width = queries.shape
    kv_heads = kv_here.shape[0]
    group = heads // kv_heads
    shards = ids.shape[0]
    chips = shards // 2
    rows = tokens * group
    length = tokens * shards
    bf16, f32 = jnp.bfloat16, jnp.float32
    vmem = pl.BlockSpec(memory_space=pltpu.VMEM)
    anywhere = pl.BlockSpec(memory_space=pl.ANY)
    dma = pltpu.SemaphoreType.DMA
    piece = (2, tokens, width)
    block = pltpu.VMEM((kv_heads, tokens, group, width), bf16)
    hop = pltpu.VMEM((kv_heads, chips) + piece, bf16)
    return pl.pallas_call(
        fused_kernel,
        in_specs=[vmem, vmem, anywhere, anywhere],
        out_specs=[anywhere, anywhere, vmem],
        out_shape=[
            jax.ShapeDtypeStruct(queries.shape, bf16),
            jax.ShapeDtypeStruct(queries.shape, bf16),
            jax.ShapeDtypeStruct(kv_here.shape, bf16),
        ],
        scratch_shapes=[block] * 4
        + [pltpu.VMEM((kv_heads, 2, chips) + piece, bf16)] * 2
        + [hop] * 5
        + [
            pltpu.VMEM(ids.shape, jnp.int32),
            pltpu.VMEM((length // BLK, rows), f32),
            pltpu.VMEM((length, rows), f32),
            pltpu.VMEM((length, rows), bf16),
        ]
        + [dma((kv_heads,))] * 4
        + [dma((shards,))] * 2
        + [dma((kv_heads, chips))] * 6
        + [dma((kv_heads,))] * 2
        + [dma((kv_heads, chips))] * 4,
        compiler_params=pltpu.CompilerParams(
            collective_id=0, has_side_effects=True, vmem_limit_bytes=60 * 1024 * 1024
        ),
        name="fused",
    )(ids, kv_here, queries, out_grad)


def lane_ids(rand_blocks, global_blocks, shards, here):
    group, block_count, slots = rand_blocks.shape
    ids = rand_blocks.reshape(group, shards, here, slots).transpose(1, 2, 3, 0)
    ids = ids.reshape(shards, here * slots, 1, group)
    reps = 128 // group
    ids = jnp.broadcast_to(ids, (shards, here * slots, reps, group)).reshape(shards, here * slots, 128)
    common = jnp.broadcast_to(global_blocks[None, :, None], (shards, global_blocks.shape[0], 128))
    return jnp.concatenate([ids, common], axis=1)


def body(shards, queries, keys, values, out_grad, rand_blocks, global_blocks):
    tokens, kv_heads, width = keys.shape
    here = tokens // BLK
    block_count = rand_blocks.shape[1]
    group = queries.shape[1] // kv_heads
    me = lax.axis_index("ctx")
    if (shards == kv_heads == group == 8 and here == 2 and rand_blocks.shape[2] == 3
            and global_blocks.shape[0] == 2):
        kv_here = jnp.stack([keys.transpose(1, 0, 2), values.transpose(1, 0, 2)], axis=1)
        ids = lane_ids(rand_blocks, global_blocks, shards, here)
        output, query_grad, sums = fused(queries, out_grad, kv_here, ids)
        grads = sums.transpose(1, 2, 0, 3)
        return output, query_grad, grads[0], grads[1]
    kv_here = jnp.stack([keys.transpose(1, 0, 2), values.transpose(1, 0, 2)], axis=1)
    kv = lax.all_gather(kv_here, "ctx", axis=0)
    rand_all = lax.all_gather(rand_blocks, "ctx", axis=0, tiled=True)
    bias = row_bias(rand_all, global_blocks, me * here, here, block_count, kv_heads)
    output, query_grad, parts = local_attention(queries, out_grad, kv, bias)
    sums = lax.psum_scatter(parts, "ctx", scatter_dimension=0, tiled=False)
    grads = sums.transpose(1, 2, 0, 3)
    return output, query_grad, grads[0], grads[1]


def solution(mesh):
    split = P(("dp", "ctx"), None, None)
    return jax.shard_map(
        functools.partial(body, mesh.shape["ctx"]),
        mesh=mesh,
        in_specs=(split, split, split, split, split, P("dp")),
        out_specs=(split, split, split, split),
        check_vma=False,
    )
```

```python
import functools
import math

import jax
import jax.numpy as jnp
from jax import lax
from jax.experimental import pallas as pl
from jax.experimental.pallas import tpu as pltpu
from jax.sharding import PartitionSpec as P

BLK = 64
NT = (((1,), (1,)), ((), ()))
NN = (((1,), (0,)), ((), ()))


def dot(left, right, dims=NN):
    return lax.dot_general(left, right, dims, preferred_element_type=jnp.float32)


def flat_rows(block):
    rows = block.shape[0] * block.shape[1]
    return block.astype(jnp.float32).reshape(rows, block.shape[2])


def for_chunks(count, step, init):
    return lax.fori_loop(0, count, step, init, unroll=count <= 4)


def attention(geometry, q_ref, g_ref, kv_ref, bias_ref, out_ref, dq_ref, dkv_ref, s_buf, e_buf, acc):
    chunk, row_tile = geometry
    shards, _, _, shard_tokens, width = kv_ref.shape
    length = shards * shard_tokens
    count = length // chunk
    tokens, group, _ = q_ref.shape
    rows = tokens * group
    tiles = rows // row_tile
    tile_tokens = row_tile // group
    factor = 1.0 / math.sqrt(width)
    to_log2 = factor * math.log2(math.e)
    per_chunk = chunk // shard_tokens

    def kv_chunk(which, c):
        return kv_ref[pl.ds(c * per_chunk, per_chunk), 0, which].reshape(chunk, width)

    for tile in range(tiles):
        t0 = tile * tile_tokens
        lanes = pl.ds(tile * row_tile, row_tile)
        q = flat_rows(q_ref[pl.ds(t0, tile_tokens)]).astype(jnp.bfloat16)
        g32 = flat_rows(g_ref[pl.ds(t0, tile_tokens)])

        def score_step(c, top):
            s = dot(kv_chunk(0, c), q, NT) * to_log2
            blocks = chunk // BLK
            bias = bias_ref[0, pl.ds(c * blocks, blocks), :, lanes]
            s = (s.reshape(blocks, BLK, row_tile) + bias).reshape(chunk, row_tile)
            s_buf[pl.ds(c * chunk, chunk)] = s
            return jnp.maximum(top, jnp.max(s, axis=0, keepdims=True))

        top = for_chunks(count, score_step, jnp.full((1, row_tile), -jnp.inf, jnp.float32))

        def weight_step(c, carry):
            total, out_t = carry
            e = jnp.exp2(s_buf[pl.ds(c * chunk, chunk)] - top)
            total = total + jnp.sum(e, axis=0, keepdims=True)
            e16 = e.astype(jnp.bfloat16)
            e_buf[pl.ds(c * chunk, chunk)] = e16
            out_t = out_t + dot(kv_chunk(1, c).T, e16)
            return total, out_t

        total, out_t = for_chunks(
            count,
            weight_step,
            (jnp.zeros((1, row_tile), jnp.float32), jnp.zeros((width, row_tile), jnp.float32)),
        )
        inverse = 1.0 / total
        out16 = (out_t * inverse).T.astype(jnp.bfloat16)
        out32 = out16.astype(jnp.float32)
        out_ref[pl.ds(t0, tile_tokens)] = out32.reshape(tile_tokens, group, width).astype(jnp.bfloat16)
        delta = jnp.sum((g32 * out32).T, axis=0, keepdims=True) * inverse
        g16 = (g32.T * inverse).T.astype(jnp.bfloat16)

        def grad_step(c, dq_t):
            at = pl.ds(c * chunk, chunk)
            e16 = e_buf[at]
            dp = dot(kv_chunk(1, c), g16, NT)
            ds = (e16.astype(jnp.float32) * (dp - delta)).astype(jnp.bfloat16)
            dk = dot(ds, q)
            dv = dot(e16, g16)
            if tile > 0:
                dk = dk + acc[0, at]
                dv = dv + acc[1, at]
            if tile < tiles - 1:
                acc[0, at] = dk
                acc[1, at] = dv
            else:
                shape = (per_chunk, shard_tokens, width)
                spot = pl.ds(c * per_chunk, per_chunk)
                dkv_ref[spot, 0, 0] = (dk * factor).astype(jnp.bfloat16).reshape(shape)
                dkv_ref[spot, 0, 1] = dv.astype(jnp.bfloat16).reshape(shape)
            return dq_t + dot(kv_chunk(0, c).T, ds)

        dq_t = for_chunks(count, grad_step, jnp.zeros((width, row_tile), jnp.float32))
        dq = (dq_t * factor).T.reshape(tile_tokens, group, width)
        dq_ref[pl.ds(t0, tile_tokens)] = dq.astype(jnp.bfloat16)


def local_attention(queries, out_grad, kv, bias):
    tokens, heads, width = queries.shape
    shards, kv_heads, _, shard_tokens, _ = kv.shape
    group = heads // kv_heads
    length = shards * shard_tokens
    rows = tokens * group
    chunk = math.gcd(length, 256)
    row_tile = rows
    while row_tile * length > (1 << 21) and row_tile > 128:
        row_tile //= 2
    acc_rows = length if row_tile < rows else 8
    blocks = length // BLK
    q_spec = pl.BlockSpec((tokens, group, width), lambda g: (0, g, 0))
    kv_spec = pl.BlockSpec((shards, 1, 2, shard_tokens, width), lambda g: (0, g, 0, 0, 0))
    return pl.pallas_call(
        functools.partial(attention, (chunk, row_tile)),
        grid=(kv_heads,),
        in_specs=[
            q_spec,
            q_spec,
            kv_spec,
            pl.BlockSpec((1, blocks, 1, rows), lambda g: (g, 0, 0, 0)),
        ],
        out_specs=[q_spec, q_spec, kv_spec],
        out_shape=[
            jax.ShapeDtypeStruct(queries.shape, jnp.bfloat16),
            jax.ShapeDtypeStruct(queries.shape, jnp.bfloat16),
            jax.ShapeDtypeStruct(kv.shape, jnp.bfloat16),
        ],
        scratch_shapes=[
            pltpu.VMEM((length, row_tile), jnp.float32),
            pltpu.VMEM((length, row_tile), jnp.bfloat16),
            pltpu.VMEM((2, acc_rows, width), jnp.float32),
        ],
        compiler_params=pltpu.CompilerParams(vmem_limit_bytes=60 * 1024 * 1024),
        name="attention",
    )(queries, out_grad, kv, bias)


def row_bias(rand_all, global_blocks, first, here, block_count, kv_heads):
    heads = rand_all.shape[0]
    group = heads // kv_heads
    mine = lax.dynamic_slice_in_dim(rand_all, first, here, axis=1)
    ids = first + jnp.arange(here, dtype=jnp.int32)
    key_ids = jnp.arange(block_count, dtype=jnp.int32)
    away = (key_ids[None, :] - ids[:, None] + block_count + 1) % block_count
    common = (away <= 2) | jnp.any(key_ids[None, :, None] == global_blocks[None, None, :], axis=2)
    chosen = jnp.any(mine[:, :, None, :] == key_ids[None, None, :, None], axis=3)
    live = chosen | common[None]
    bias = jnp.where(live, 0.0, -jnp.inf).astype(jnp.float32)
    bias = bias.reshape(kv_heads, group, here, block_count).transpose(0, 3, 2, 1)
    bias = jnp.broadcast_to(bias[:, :, :, None, :], (kv_heads, block_count, here, BLK, group))
    return bias.reshape(kv_heads, block_count, 1, here * BLK * group)


def fused_kernel(
    ids_in, k_in, v_in, q_hbm, g_hbm, out_hbm, dq_hbm, dk_ref, dv_ref, grads_ref,
    q_buf, g_buf, o_buf, dq_buf, kv_buf, part_buf, sib_in, right_in, left_in, right_out, left_out,
    ids_buf, bias_buf, s_buf, e_buf,
    q_sem, g_sem, o_sem, dq_sem,
    ids_send, ids_recv, sib_send, sib_recv, fwd_send, fwd_recv, back_send, back_recv,
    pair_send, pair_recv, right_send, right_recv, left_send, left_recv,
):
    heads, _, chips, _, shard_tokens, width = kv_buf.shape
    shards = 2 * chips
    _, tokens, group, _ = q_buf.shape
    rows = tokens * group
    here = tokens // BLK
    block_count = shards * here
    half = BLK * group
    factor = 1.0 / math.sqrt(width)
    to_log2 = factor * math.log2(math.e)
    me = lax.axis_index("ctx")
    z, core = me // 2, me % 2
    pair = z * 2 + 1 - core
    ahead, behind = me + 2, me - 2
    last = chips - 1

    def send(source, target, send_sem, recv_sem, to):
        return pltpu.make_async_remote_copy(
            src_ref=source, dst_ref=target, send_sem=send_sem, recv_sem=recv_sem,
            device_id={"ctx": to}, device_id_type=pl.DeviceIdType.MESH,
        )

    def send_ids(k):
        to = lax.rem(me + k, shards)
        return send(ids_in.at[to], ids_buf.at[me], ids_send.at[k], ids_recv.at[me], to)

    def got_ids(k):
        origin = lax.rem(me + k, shards)
        return send(ids_in.at[origin], ids_buf.at[origin], ids_send.at[k], ids_recv.at[origin], origin)

    def kv_move(h, origin, lane, sems, to):
        spot = kv_buf.at[h, lane, origin]
        return send(spot, spot, sems[0].at[h, origin], sems[1].at[h, origin], to)

    sib_sems, fwd_sems, back_sems = (sib_send, sib_recv), (fwd_send, fwd_recv), (back_send, back_recv)

    def pair_move(h):
        return send(part_buf.at[h, 1 - core], sib_in.at[h], pair_send.at[h], pair_recv.at[h], pair)

    def right_move(h, zd):
        return send(right_out.at[h, zd], right_in.at[h, zd], right_send.at[h, zd], right_recv.at[h, zd], ahead)

    def left_move(h, zd):
        return send(left_out.at[h, zd], left_in.at[h, zd], left_send.at[h, zd], left_recv.at[h, zd], behind)

    def head_columns(ref, h):
        return ref.at[:, pl.ds(pl.multiple_of(h * group, group), group), :]

    def load_q(h):
        return pltpu.make_async_copy(head_columns(q_hbm, h), q_buf.at[h], q_sem.at[h])

    def load_g(h):
        return pltpu.make_async_copy(head_columns(g_hbm, h), g_buf.at[h], g_sem.at[h])

    def store_o(h):
        return pltpu.make_async_copy(o_buf.at[h], head_columns(out_hbm, h), o_sem.at[h])

    def store_dq(h):
        return pltpu.make_async_copy(dq_buf.at[h], head_columns(dq_hbm, h), dq_sem.at[h])

    def each_head(step):
        def run(h, carry):
            step(h)
            return carry
        lax.fori_loop(0, heads, run, 0)

    def start_loads(h):
        load_q(h).start()
        load_g(h).start()

    each_head(start_loads)
    for which, ref in enumerate((k_in, v_in)):
        turned = jnp.swapaxes(ref[...].astype(jnp.float32), 0, 1)
        kv_buf[:, core, z, which] = turned.astype(jnp.bfloat16)
    ids_buf[me] = ids_in[me]

    barrier = pltpu.get_barrier_semaphore()
    for k in range(1, shards):
        pl.semaphore_signal(
            barrier, inc=1, device_id={"ctx": lax.rem(me + k, shards)}, device_id_type=pl.DeviceIdType.MESH
        )
    pl.semaphore_wait(barrier, shards - 1)

    def forward_kv(h, origin, rightward, leftward):
        @pl.when(rightward)
        def _():
            kv_move(h, origin, core, fwd_sems, ahead).start()

        @pl.when(leftward)
        def _():
            kv_move(h, origin, core, back_sems, behind).start()

        kv_move(h, origin, core, sib_sems, pair).start()

    def both(h):
        return part_buf[h, core].astype(jnp.float32), sib_in[h].astype(jnp.float32)

    def combined(h, zd):
        return part_buf[h, core, zd].astype(jnp.float32) + sib_in[h, zd].astype(jnp.float32)

    def in_heads(h):
        return jnp.logical_and(h >= 0, h < heads)

    def reduce_right(h):
        for zd in range(chips - 1, 0, -1):
            @pl.when(zd > z)
            def _(zd=zd):
                @pl.when(z == 0)
                def _():
                    right_out[h, zd] = combined(h, zd).astype(jnp.bfloat16)

                @pl.when(z > 0)
                def _():
                    right_move(h, zd).wait_recv()
                    total = combined(h, zd) + right_in[h, zd].astype(jnp.float32)
                    right_out[h, zd] = total.astype(jnp.bfloat16)

                right_move(h, zd).start()

    def reduce_left(h):
        for zd in range(chips - 1):
            @pl.when(zd < z)
            def _(zd=zd):
                @pl.when(z == last)
                def _():
                    left_out[h, zd] = combined(h, zd).astype(jnp.bfloat16)

                @pl.when(z < last)
                def _():
                    left_move(h, zd).wait_recv()
                    total = combined(h, zd) + left_in[h, zd].astype(jnp.float32)
                    left_out[h, zd] = total.astype(jnp.bfloat16)

                left_move(h, zd).start()

    def finish(h):
        @pl.when(z > 0)
        def _():
            right_move(h, z).wait_recv()

        @pl.when(z < last)
        def _():
            left_move(h, z).wait_recv()

        @pl.when(z == 0)
        def _():
            grads_ref[h] = (combined(h, z) + left_in[h, z].astype(jnp.float32)).astype(jnp.bfloat16)

        @pl.when(z == last)
        def _():
            grads_ref[h] = (combined(h, z) + right_in[h, z].astype(jnp.float32)).astype(jnp.bfloat16)

        @pl.when(jnp.logical_and(z > 0, z < last))
        def _():
            arrived = right_in[h, z].astype(jnp.float32) + left_in[h, z].astype(jnp.float32)
            grads_ref[h] = (combined(h, z) + arrived).astype(jnp.bfloat16)

    def compute(h):
        load_q(h).wait()
        load_g(h).wait()
        q = flat_rows(q_buf[h]).astype(jnp.bfloat16)
        g32 = flat_rows(g_buf[h])
        ids = ids_buf[h]
        key_ids = lax.broadcasted_iota(jnp.int32, (block_count, ids.shape[1]), 0)
        slots = (ids.shape[0] - 2) // here
        for b in range(here):
            away = key_ids - (me * here + b) + (block_count + 1)
            for _ in range(2):
                away = jnp.where(away >= block_count, away - block_count, away)
            live = (away <= 2) | (key_ids == ids[6:7]) | (key_ids == ids[7:8])
            for k in range(slots):
                live = live | (key_ids == ids[b * slots + k:b * slots + k + 1])
            bias = jnp.where(live, 0.0, -jnp.inf).astype(jnp.float32)
            reps = half // ids.shape[1]
            bias_buf[:, b * half:(b + 1) * half] = jnp.concatenate([bias] * reps, axis=1)

        chunk = 2 * shard_tokens
        spans = [(lane, zz) for lane in range(2) for zz in range(0, chips, 2)]

        def kv_chunk(which, span):
            return kv_buf[h, span[0], span[1]:span[1] + 2, which].reshape(chunk, width)

        top = None
        for c, span in enumerate(spans):
            s = dot(kv_chunk(0, span), q, NT) * to_log2
            pieces = []
            for j in range(2 * here):
                block = ((span[1] + j // here) * 2 + span[0]) * here + j % here
                pieces.append(s[j * BLK:(j + 1) * BLK] + bias_buf[block:block + 1])
            s = jnp.concatenate(pieces, axis=0)
            s_buf[c * chunk:(c + 1) * chunk] = s
            here_top = jnp.max(s, axis=0, keepdims=True)
            top = here_top if top is None else jnp.maximum(top, here_top)

        total = jnp.zeros((1, rows), jnp.float32)
        out_t = jnp.zeros((width, rows), jnp.float32)
        for c, span in enumerate(spans):
            e = jnp.exp2(s_buf[c * chunk:(c + 1) * chunk] - top)
            total = total + jnp.sum(e, axis=0, keepdims=True)
            e16 = e.astype(jnp.bfloat16)
            e_buf[c * chunk:(c + 1) * chunk] = e16
            out_t = out_t + dot(kv_chunk(1, span).T, e16)
        inverse = 1.0 / total
        out16 = (out_t * inverse).T.astype(jnp.bfloat16)
        out32 = out16.astype(jnp.float32)
        o_buf[h] = out32.reshape(tokens, group, width).astype(jnp.bfloat16)
        store_o(h).start()
        delta = jnp.sum((g32 * out32).T, axis=0, keepdims=True) * inverse
        g16 = (g32.T * inverse).T.astype(jnp.bfloat16)

        dq_t = jnp.zeros((width, rows), jnp.float32)
        for c, span in enumerate(spans):
            e16 = e_buf[c * chunk:(c + 1) * chunk]
            dp = dot(kv_chunk(1, span), g16, NT)
            ds = (e16.astype(jnp.float32) * (dp - delta)).astype(jnp.bfloat16)
            shape = (2, shard_tokens, width)
            dk = (dot(ds, q) * factor).astype(jnp.bfloat16)
            dv = dot(e16, g16).astype(jnp.bfloat16)
            part_buf[h, span[0], span[1]:span[1] + 2, 0] = dk.reshape(shape)
            part_buf[h, span[0], span[1]:span[1] + 2, 1] = dv.reshape(shape)
            dq_t = dq_t + dot(kv_chunk(0, span).T, ds)
        pair_move(h).start()
        dq = (dq_t * factor).T.reshape(tokens, group, width)
        dq_buf[h] = dq.astype(jnp.bfloat16)
        store_dq(h).start()

    lag = chips - 1

    def slot(t, carry):
        for d in range(chips - 1, 0, -1):
            h = t - d

            @pl.when(in_heads(h))
            def _(h=h, d=d):
                @pl.when(z - d >= 0)
                def _():
                    kv_move(h, z - d, core, fwd_sems, ahead).wait_recv()
                    forward_kv(h, z - d, z < last, z < 0)

                @pl.when(z + d <= last)
                def _():
                    kv_move(h, z + d, core, back_sems, behind).wait_recv()
                    forward_kv(h, z + d, z < 0, z > 0)

        @pl.when(t < heads)
        def _():
            forward_kv(t, z, z < last, z > 0)

        @pl.when(t == 0)
        def _():
            for k in range(1, shards):
                send_ids(k).start()

        e = t - lag - 1

        @pl.when(in_heads(e))
        def _():
            pair_move(e).wait_recv()

        @pl.when(jnp.logical_and(in_heads(e - z), z < last))
        def _():
            reduce_right(e - z)

        @pl.when(jnp.logical_and(in_heads(e - (last - z)), z > 0))
        def _():
            reduce_left(e - (last - z))

        f = e - jnp.maximum(z, last - z)

        @pl.when(in_heads(f))
        def _():
            finish(f)

        @pl.when(t == lag)
        def _():
            for k in range(1, shards):
                got_ids(k).wait_recv()

        @pl.when(in_heads(t - lag))
        def _():
            for origin in range(chips):
                kv_move(t - lag, origin, 1 - core, sib_sems, pair).wait_recv()
            compute(t - lag)

        return carry

    lax.fori_loop(0, heads + lag + chips, slot, 0)

    for which, ref in enumerate((dk_ref, dv_ref)):
        turned = jnp.swapaxes(grads_ref[:, which].astype(jnp.float32), 0, 1)
        ref[...] = turned.astype(jnp.bfloat16)

    for k in range(1, shards):
        send_ids(k).wait_send()

    def drain(h):
        store_o(h).wait()
        store_dq(h).wait()
        pair_move(h).wait_send()
        for origin in range(chips):
            kv_move(h, origin, core, sib_sems, pair).wait_send()

            @pl.when(jnp.logical_and(origin <= z, z < last))
            def _(origin=origin):
                kv_move(h, origin, core, fwd_sems, ahead).wait_send()

            @pl.when(jnp.logical_and(origin >= z, z > 0))
            def _(origin=origin):
                kv_move(h, origin, core, back_sems, behind).wait_send()

            @pl.when(origin > z)
            def _(origin=origin):
                right_move(h, origin).wait_send()

            @pl.when(origin < z)
            def _(origin=origin):
                left_move(h, origin).wait_send()

    each_head(drain)


def fused(queries, out_grad, keys, values, ids):
    tokens, heads, width = queries.shape
    kv_heads = keys.shape[1]
    group = heads // kv_heads
    shards = ids.shape[0]
    chips = shards // 2
    rows = tokens * group
    length = tokens * shards
    bf16, f32 = jnp.bfloat16, jnp.float32
    vmem = pl.BlockSpec(memory_space=pltpu.VMEM)
    anywhere = pl.BlockSpec(memory_space=pl.ANY)
    dma = pltpu.SemaphoreType.DMA
    piece = (2, tokens, width)
    block = pltpu.VMEM((kv_heads, tokens, group, width), bf16)
    hop = pltpu.VMEM((kv_heads, chips) + piece, bf16)
    return pl.pallas_call(
        fused_kernel,
        in_specs=[vmem, vmem, vmem, anywhere, anywhere],
        out_specs=[anywhere, anywhere, vmem, vmem],
        out_shape=[
            jax.ShapeDtypeStruct(queries.shape, bf16),
            jax.ShapeDtypeStruct(queries.shape, bf16),
            jax.ShapeDtypeStruct(keys.shape, bf16),
            jax.ShapeDtypeStruct(keys.shape, bf16),
        ],
        scratch_shapes=[pltpu.VMEM((kv_heads,) + piece, bf16)] + [block] * 4
        + [pltpu.VMEM((kv_heads, 2, chips) + piece, bf16)] * 2
        + [hop] * 5
        + [
            pltpu.VMEM(ids.shape, jnp.int32),
            pltpu.VMEM((length // BLK, rows), f32),
            pltpu.VMEM((length, rows), f32),
            pltpu.VMEM((length, rows), bf16),
        ]
        + [dma((kv_heads,))] * 4
        + [dma((shards,))] * 2
        + [dma((kv_heads, chips))] * 6
        + [dma((kv_heads,))] * 2
        + [dma((kv_heads, chips))] * 4,
        compiler_params=pltpu.CompilerParams(
            collective_id=0, has_side_effects=True, vmem_limit_bytes=60 * 1024 * 1024
        ),
        name="fused",
    )(ids, keys, values, queries, out_grad)


def lane_ids(rand_blocks, global_blocks, shards, here):
    group, block_count, slots = rand_blocks.shape
    ids = rand_blocks.reshape(group, shards, here, slots).transpose(1, 2, 3, 0)
    ids = ids.reshape(shards, here * slots, 1, group)
    reps = 128 // group
    ids = jnp.broadcast_to(ids, (shards, here * slots, reps, group)).reshape(shards, here * slots, 128)
    common = jnp.broadcast_to(global_blocks[None, :, None], (shards, global_blocks.shape[0], 128))
    return jnp.concatenate([ids, common], axis=1)


def body(shards, queries, keys, values, out_grad, rand_blocks, global_blocks):
    tokens, kv_heads, width = keys.shape
    here = tokens // BLK
    block_count = rand_blocks.shape[1]
    group = queries.shape[1] // kv_heads
    me = lax.axis_index("ctx")
    if (shards == kv_heads == group == 8 and here == 2 and rand_blocks.shape[2] == 3
            and global_blocks.shape[0] == 2):
        ids = lane_ids(rand_blocks, global_blocks, shards, here)
        return fused(queries, out_grad, keys, values, ids)
    kv_here = jnp.stack([keys.transpose(1, 0, 2), values.transpose(1, 0, 2)], axis=1)
    kv = lax.all_gather(kv_here, "ctx", axis=0)
    rand_all = lax.all_gather(rand_blocks, "ctx", axis=0, tiled=True)
    bias = row_bias(rand_all, global_blocks, me * here, here, block_count, kv_heads)
    output, query_grad, parts = local_attention(queries, out_grad, kv, bias)
    sums = lax.psum_scatter(parts, "ctx", scatter_dimension=0, tiled=False)
    grads = sums.transpose(1, 2, 0, 3)
    return output, query_grad, grads[0], grads[1]


def solution(mesh):
    split = P(("dp", "ctx"), None, None)
    return jax.shard_map(
        functools.partial(body, mesh.shape["ctx"]),
        mesh=mesh,
        in_specs=(split, split, split, split, split, P("dp")),
        out_specs=(split, split, split, split),
        check_vma=False,
    )
```

```python
import functools
import math

import jax
import jax.numpy as jnp
from jax import lax
from jax.experimental import pallas as pl
from jax.experimental.pallas import tpu as pltpu
from jax.sharding import PartitionSpec as P

BLK = 64
NT = (((1,), (1,)), ((), ()))
NN = (((1,), (0,)), ((), ()))


def dot(left, right, dims=NN):
    return lax.dot_general(left, right, dims, preferred_element_type=jnp.float32)


def flat_rows(block):
    rows = block.shape[0] * block.shape[1]
    return block.astype(jnp.float32).reshape(rows, block.shape[2])


def for_chunks(count, step, init):
    return lax.fori_loop(0, count, step, init, unroll=count <= 4)


def attention(geometry, q_ref, g_ref, kv_ref, bias_ref, out_ref, dq_ref, dkv_ref, s_buf, e_buf, acc):
    chunk, row_tile = geometry
    shards, _, _, shard_tokens, width = kv_ref.shape
    length = shards * shard_tokens
    count = length // chunk
    tokens, group, _ = q_ref.shape
    rows = tokens * group
    tiles = rows // row_tile
    tile_tokens = row_tile // group
    factor = 1.0 / math.sqrt(width)
    to_log2 = factor * math.log2(math.e)
    per_chunk = chunk // shard_tokens

    def kv_chunk(which, c):
        return kv_ref[pl.ds(c * per_chunk, per_chunk), 0, which].reshape(chunk, width)

    for tile in range(tiles):
        t0 = tile * tile_tokens
        lanes = pl.ds(tile * row_tile, row_tile)
        q = flat_rows(q_ref[pl.ds(t0, tile_tokens)]).astype(jnp.bfloat16)
        g32 = flat_rows(g_ref[pl.ds(t0, tile_tokens)])

        def score_step(c, top):
            s = dot(kv_chunk(0, c), q, NT) * to_log2
            blocks = chunk // BLK
            bias = bias_ref[0, pl.ds(c * blocks, blocks), :, lanes]
            s = (s.reshape(blocks, BLK, row_tile) + bias).reshape(chunk, row_tile)
            s_buf[pl.ds(c * chunk, chunk)] = s
            return jnp.maximum(top, jnp.max(s, axis=0, keepdims=True))

        top = for_chunks(count, score_step, jnp.full((1, row_tile), -jnp.inf, jnp.float32))

        def weight_step(c, carry):
            total, out_t = carry
            e = jnp.exp2(s_buf[pl.ds(c * chunk, chunk)] - top)
            total = total + jnp.sum(e, axis=0, keepdims=True)
            e16 = e.astype(jnp.bfloat16)
            e_buf[pl.ds(c * chunk, chunk)] = e16
            out_t = out_t + dot(kv_chunk(1, c).T, e16)
            return total, out_t

        total, out_t = for_chunks(
            count,
            weight_step,
            (jnp.zeros((1, row_tile), jnp.float32), jnp.zeros((width, row_tile), jnp.float32)),
        )
        inverse = 1.0 / total
        out16 = (out_t * inverse).T.astype(jnp.bfloat16)
        out32 = out16.astype(jnp.float32)
        out_ref[pl.ds(t0, tile_tokens)] = out32.reshape(tile_tokens, group, width).astype(jnp.bfloat16)
        delta = jnp.sum((g32 * out32).T, axis=0, keepdims=True) * inverse
        g16 = (g32.T * inverse).T.astype(jnp.bfloat16)

        def grad_step(c, dq_t):
            at = pl.ds(c * chunk, chunk)
            e16 = e_buf[at]
            dp = dot(kv_chunk(1, c), g16, NT)
            ds = (e16.astype(jnp.float32) * (dp - delta)).astype(jnp.bfloat16)
            dk = dot(ds, q)
            dv = dot(e16, g16)
            if tile > 0:
                dk = dk + acc[0, at]
                dv = dv + acc[1, at]
            if tile < tiles - 1:
                acc[0, at] = dk
                acc[1, at] = dv
            else:
                shape = (per_chunk, shard_tokens, width)
                spot = pl.ds(c * per_chunk, per_chunk)
                dkv_ref[spot, 0, 0] = (dk * factor).astype(jnp.bfloat16).reshape(shape)
                dkv_ref[spot, 0, 1] = dv.astype(jnp.bfloat16).reshape(shape)
            return dq_t + dot(kv_chunk(0, c).T, ds)

        dq_t = for_chunks(count, grad_step, jnp.zeros((width, row_tile), jnp.float32))
        dq = (dq_t * factor).T.reshape(tile_tokens, group, width)
        dq_ref[pl.ds(t0, tile_tokens)] = dq.astype(jnp.bfloat16)


def local_attention(queries, out_grad, kv, bias):
    tokens, heads, width = queries.shape
    shards, kv_heads, _, shard_tokens, _ = kv.shape
    group = heads // kv_heads
    length = shards * shard_tokens
    rows = tokens * group
    chunk = math.gcd(length, 256)
    row_tile = rows
    while row_tile * length > (1 << 21) and row_tile > 128:
        row_tile //= 2
    acc_rows = length if row_tile < rows else 8
    blocks = length // BLK
    q_spec = pl.BlockSpec((tokens, group, width), lambda g: (0, g, 0))
    kv_spec = pl.BlockSpec((shards, 1, 2, shard_tokens, width), lambda g: (0, g, 0, 0, 0))
    return pl.pallas_call(
        functools.partial(attention, (chunk, row_tile)),
        grid=(kv_heads,),
        in_specs=[
            q_spec,
            q_spec,
            kv_spec,
            pl.BlockSpec((1, blocks, 1, rows), lambda g: (g, 0, 0, 0)),
        ],
        out_specs=[q_spec, q_spec, kv_spec],
        out_shape=[
            jax.ShapeDtypeStruct(queries.shape, jnp.bfloat16),
            jax.ShapeDtypeStruct(queries.shape, jnp.bfloat16),
            jax.ShapeDtypeStruct(kv.shape, jnp.bfloat16),
        ],
        scratch_shapes=[
            pltpu.VMEM((length, row_tile), jnp.float32),
            pltpu.VMEM((length, row_tile), jnp.bfloat16),
            pltpu.VMEM((2, acc_rows, width), jnp.float32),
        ],
        compiler_params=pltpu.CompilerParams(vmem_limit_bytes=60 * 1024 * 1024),
        name="attention",
    )(queries, out_grad, kv, bias)


def row_bias(rand_all, global_blocks, first, here, block_count, kv_heads):
    heads = rand_all.shape[0]
    group = heads // kv_heads
    mine = lax.dynamic_slice_in_dim(rand_all, first, here, axis=1)
    ids = first + jnp.arange(here, dtype=jnp.int32)
    key_ids = jnp.arange(block_count, dtype=jnp.int32)
    away = (key_ids[None, :] - ids[:, None] + block_count + 1) % block_count
    common = (away <= 2) | jnp.any(key_ids[None, :, None] == global_blocks[None, None, :], axis=2)
    chosen = jnp.any(mine[:, :, None, :] == key_ids[None, None, :, None], axis=3)
    live = chosen | common[None]
    bias = jnp.where(live, 0.0, -jnp.inf).astype(jnp.float32)
    bias = bias.reshape(kv_heads, group, here, block_count).transpose(0, 3, 2, 1)
    bias = jnp.broadcast_to(bias[:, :, :, None, :], (kv_heads, block_count, here, BLK, group))
    return bias.reshape(kv_heads, block_count, 1, here * BLK * group)


def fused_kernel(
    ids_in, k_in, v_in, q_hbm, g_hbm, out_hbm, dq_hbm, dk_ref, dv_ref, grads_ref,
    q_buf, g_buf, o_buf, dq_buf, kv_buf, part_buf, sib_in, right_in, left_in, right_out, left_out,
    ids_buf, bias_buf, s_buf, e_buf,
    q_sem, g_sem, o_sem, dq_sem,
    ids_send, ids_recv, sib_send, sib_recv, fwd_send, fwd_recv, back_send, back_recv,
    pair_send, pair_recv, right_send, right_recv, left_send, left_recv,
):
    heads, _, chips, _, shard_tokens, width = kv_buf.shape
    shards = 2 * chips
    _, tokens, group, _ = q_buf.shape
    rows = tokens * group
    here = tokens // BLK
    block_count = shards * here
    half = BLK * group
    factor = 1.0 / math.sqrt(width)
    to_log2 = factor * math.log2(math.e)
    me = lax.axis_index("ctx")
    z, core = me // 2, me % 2
    pair = z * 2 + 1 - core
    ahead, behind = me + 2, me - 2
    last = chips - 1

    def send(source, target, send_sem, recv_sem, to):
        return pltpu.make_async_remote_copy(
            src_ref=source, dst_ref=target, send_sem=send_sem, recv_sem=recv_sem,
            device_id={"ctx": to}, device_id_type=pl.DeviceIdType.MESH,
        )

    def send_ids(k):
        to = lax.rem(me + k, shards)
        return send(ids_in.at[to], ids_buf.at[me], ids_send.at[k], ids_recv.at[me], to)

    def got_ids(k):
        origin = lax.rem(me + k, shards)
        return send(ids_in.at[origin], ids_buf.at[origin], ids_send.at[k], ids_recv.at[origin], origin)

    def kv_move(h, origin, lane, sems, to):
        spot = kv_buf.at[h, lane, origin]
        return send(spot, spot, sems[0].at[h, origin], sems[1].at[h, origin], to)

    sib_sems, fwd_sems, back_sems = (sib_send, sib_recv), (fwd_send, fwd_recv), (back_send, back_recv)

    def pair_move(h):
        return send(part_buf.at[h, 1 - core], sib_in.at[h], pair_send.at[h], pair_recv.at[h], pair)

    def right_move(h, zd):
        return send(right_out.at[h, zd], right_in.at[h, zd], right_send.at[h, zd], right_recv.at[h, zd], ahead)

    def left_move(h, zd):
        return send(left_out.at[h, zd], left_in.at[h, zd], left_send.at[h, zd], left_recv.at[h, zd], behind)

    def head_columns(ref, h):
        return ref.at[:, pl.ds(pl.multiple_of(h * group, group), group), :]

    def load_q(h):
        return pltpu.make_async_copy(head_columns(q_hbm, h), q_buf.at[h], q_sem.at[h])

    def load_g(h):
        return pltpu.make_async_copy(head_columns(g_hbm, h), g_buf.at[h], g_sem.at[h])

    def store_o(h):
        return pltpu.make_async_copy(o_buf.at[h], head_columns(out_hbm, h), o_sem.at[h])

    def store_dq(h):
        return pltpu.make_async_copy(dq_buf.at[h], head_columns(dq_hbm, h), dq_sem.at[h])

    def each_head(step):
        def run(h, carry):
            step(h)
            return carry
        lax.fori_loop(0, heads, run, 0)

    def start_loads(h):
        load_q(h).start()
        load_g(h).start()

    each_head(start_loads)
    for which, ref in enumerate((k_in, v_in)):
        turned = jnp.swapaxes(ref[...].astype(jnp.float32), 0, 1)
        kv_buf[:, core, z, which] = turned.astype(jnp.bfloat16)
    ids_buf[me] = ids_in[me]

    barrier = pltpu.get_barrier_semaphore()
    for k in range(1, shards):
        pl.semaphore_signal(
            barrier, inc=1, device_id={"ctx": lax.rem(me + k, shards)}, device_id_type=pl.DeviceIdType.MESH
        )
    pl.semaphore_wait(barrier, shards - 1)

    def forward_kv(h, origin, rightward, leftward):
        @pl.when(rightward)
        def _():
            kv_move(h, origin, core, fwd_sems, ahead).start()

        @pl.when(leftward)
        def _():
            kv_move(h, origin, core, back_sems, behind).start()

        kv_move(h, origin, core, sib_sems, pair).start()

    def both(h):
        return part_buf[h, core].astype(jnp.float32), sib_in[h].astype(jnp.float32)

    def combined(h, zd):
        return part_buf[h, core, zd].astype(jnp.float32) + sib_in[h, zd].astype(jnp.float32)

    def in_heads(h):
        return jnp.logical_and(h >= 0, h < heads)

    def reduce_right(h):
        for zd in range(chips - 1, 0, -1):
            @pl.when(zd > z)
            def _(zd=zd):
                @pl.when(z == 0)
                def _():
                    right_out[h, zd] = combined(h, zd).astype(jnp.bfloat16)

                @pl.when(z > 0)
                def _():
                    right_move(h, zd).wait_recv()
                    total = combined(h, zd) + right_in[h, zd].astype(jnp.float32)
                    right_out[h, zd] = total.astype(jnp.bfloat16)

                right_move(h, zd).start()

    def reduce_left(h):
        for zd in range(chips - 1):
            @pl.when(zd < z)
            def _(zd=zd):
                @pl.when(z == last)
                def _():
                    left_out[h, zd] = combined(h, zd).astype(jnp.bfloat16)

                @pl.when(z < last)
                def _():
                    left_move(h, zd).wait_recv()
                    total = combined(h, zd) + left_in[h, zd].astype(jnp.float32)
                    left_out[h, zd] = total.astype(jnp.bfloat16)

                left_move(h, zd).start()

    def finish(h):
        @pl.when(z > 0)
        def _():
            right_move(h, z).wait_recv()

        @pl.when(z < last)
        def _():
            left_move(h, z).wait_recv()

        @pl.when(z == 0)
        def _():
            grads_ref[h] = (combined(h, z) + left_in[h, z].astype(jnp.float32)).astype(jnp.bfloat16)

        @pl.when(z == last)
        def _():
            grads_ref[h] = (combined(h, z) + right_in[h, z].astype(jnp.float32)).astype(jnp.bfloat16)

        @pl.when(jnp.logical_and(z > 0, z < last))
        def _():
            arrived = right_in[h, z].astype(jnp.float32) + left_in[h, z].astype(jnp.float32)
            grads_ref[h] = (combined(h, z) + arrived).astype(jnp.bfloat16)

    def compute(h):
        load_q(h).wait()
        load_g(h).wait()
        q = flat_rows(q_buf[h]).astype(jnp.bfloat16)
        g32 = flat_rows(g_buf[h])
        ids = ids_buf[h]
        key_ids = lax.broadcasted_iota(jnp.int32, (block_count, ids.shape[1]), 0)
        slots = (ids.shape[0] - 2) // here
        for b in range(here):
            away = key_ids - (me * here + b) + (block_count + 1)
            for _ in range(2):
                away = jnp.where(away >= block_count, away - block_count, away)
            live = (away <= 2) | (key_ids == ids[6:7]) | (key_ids == ids[7:8])
            for k in range(slots):
                live = live | (key_ids == ids[b * slots + k:b * slots + k + 1])
            bias = jnp.where(live, 0.0, -jnp.inf).astype(jnp.float32)
            reps = half // ids.shape[1]
            bias_buf[:, b * half:(b + 1) * half] = jnp.concatenate([bias] * reps, axis=1)

        chunk = 2 * shard_tokens
        spans = [(lane, zz) for lane in range(2) for zz in range(0, chips, 2)]

        def kv_chunk(which, span):
            return kv_buf[h, span[0], span[1]:span[1] + 2, which].reshape(chunk, width)

        top = None
        for c, span in enumerate(spans):
            s = dot(kv_chunk(0, span), q, NT) * to_log2
            pieces = []
            for j in range(2 * here):
                block = ((span[1] + j // here) * 2 + span[0]) * here + j % here
                pieces.append(s[j * BLK:(j + 1) * BLK] + bias_buf[block:block + 1])
            s = jnp.concatenate(pieces, axis=0)
            s_buf[c * chunk:(c + 1) * chunk] = s
            here_top = jnp.max(s, axis=0, keepdims=True)
            top = here_top if top is None else jnp.maximum(top, here_top)

        total = jnp.zeros((1, rows), jnp.float32)
        out_t = jnp.zeros((width, rows), jnp.float32)
        for c, span in enumerate(spans):
            e = jnp.exp2(s_buf[c * chunk:(c + 1) * chunk] - top)
            total = total + jnp.sum(e, axis=0, keepdims=True)
            e16 = e.astype(jnp.bfloat16)
            e_buf[c * chunk:(c + 1) * chunk] = e16
            out_t = out_t + dot(kv_chunk(1, span).T, e16)
        inverse = 1.0 / total
        out16 = (out_t * inverse).T.astype(jnp.bfloat16)
        out32 = out16.astype(jnp.float32)
        o_buf[h] = out32.reshape(tokens, group, width).astype(jnp.bfloat16)
        store_o(h).start()
        delta = jnp.sum((g32 * out32).T, axis=0, keepdims=True) * inverse
        g16 = (g32.T * inverse).T.astype(jnp.bfloat16)

        dq_t = jnp.zeros((width, rows), jnp.float32)
        for k, zz in [(k, zz) for k in range(2) for zz in range(0, chips, 2)]:
            if (k, zz) == (1, 0):
                pair_move(h).start()
            span = ((1 - core) if k == 0 else core, zz)
            start = pl.multiple_of((span[0] * (chips // 2) + zz // 2) * chunk, chunk)
            e16 = e_buf[pl.ds(start, chunk)]
            dp = dot(kv_chunk(1, span), g16, NT)
            ds = (e16.astype(jnp.float32) * (dp - delta)).astype(jnp.bfloat16)
            shape = (2, shard_tokens, width)
            dk = (dot(ds, q) * factor).astype(jnp.bfloat16)
            dv = dot(e16, g16).astype(jnp.bfloat16)
            part_buf[h, span[0], span[1]:span[1] + 2, 0] = dk.reshape(shape)
            part_buf[h, span[0], span[1]:span[1] + 2, 1] = dv.reshape(shape)
            dq_t = dq_t + dot(kv_chunk(0, span).T, ds)
        dq = (dq_t * factor).T.reshape(tokens, group, width)
        dq_buf[h] = dq.astype(jnp.bfloat16)
        store_dq(h).start()

    lag = chips - 1

    def slot(t, carry):
        for d in range(chips - 1, 0, -1):
            h = t - d

            @pl.when(in_heads(h))
            def _(h=h, d=d):
                @pl.when(z - d >= 0)
                def _():
                    kv_move(h, z - d, core, fwd_sems, ahead).wait_recv()
                    forward_kv(h, z - d, z < last, z < 0)

                @pl.when(z + d <= last)
                def _():
                    kv_move(h, z + d, core, back_sems, behind).wait_recv()
                    forward_kv(h, z + d, z < 0, z > 0)

        @pl.when(t < heads)
        def _():
            forward_kv(t, z, z < last, z > 0)

        @pl.when(t == 0)
        def _():
            for k in range(1, shards):
                send_ids(k).start()

        e = t - lag - 1

        @pl.when(in_heads(e))
        def _():
            pair_move(e).wait_recv()

        @pl.when(jnp.logical_and(in_heads(e - z), z < last))
        def _():
            reduce_right(e - z)

        @pl.when(jnp.logical_and(in_heads(e - (last - z)), z > 0))
        def _():
            reduce_left(e - (last - z))

        f = e - jnp.maximum(z, last - z)

        @pl.when(in_heads(f))
        def _():
            finish(f)

        @pl.when(t == lag)
        def _():
            for k in range(1, shards):
                got_ids(k).wait_recv()

        @pl.when(in_heads(t - lag))
        def _():
            for origin in range(chips):
                kv_move(t - lag, origin, 1 - core, sib_sems, pair).wait_recv()
            compute(t - lag)

        return carry

    lax.fori_loop(0, heads + lag + chips, slot, 0)

    for which, ref in enumerate((dk_ref, dv_ref)):
        turned = jnp.swapaxes(grads_ref[:, which].astype(jnp.float32), 0, 1)
        ref[...] = turned.astype(jnp.bfloat16)

    for k in range(1, shards):
        send_ids(k).wait_send()

    def drain(h):
        store_o(h).wait()
        store_dq(h).wait()
        pair_move(h).wait_send()
        for origin in range(chips):
            kv_move(h, origin, core, sib_sems, pair).wait_send()

            @pl.when(jnp.logical_and(origin <= z, z < last))
            def _(origin=origin):
                kv_move(h, origin, core, fwd_sems, ahead).wait_send()

            @pl.when(jnp.logical_and(origin >= z, z > 0))
            def _(origin=origin):
                kv_move(h, origin, core, back_sems, behind).wait_send()

            @pl.when(origin > z)
            def _(origin=origin):
                right_move(h, origin).wait_send()

            @pl.when(origin < z)
            def _(origin=origin):
                left_move(h, origin).wait_send()

    each_head(drain)


def fused(queries, out_grad, keys, values, ids):
    tokens, heads, width = queries.shape
    kv_heads = keys.shape[1]
    group = heads // kv_heads
    shards = ids.shape[0]
    chips = shards // 2
    rows = tokens * group
    length = tokens * shards
    bf16, f32 = jnp.bfloat16, jnp.float32
    vmem = pl.BlockSpec(memory_space=pltpu.VMEM)
    anywhere = pl.BlockSpec(memory_space=pl.ANY)
    dma = pltpu.SemaphoreType.DMA
    piece = (2, tokens, width)
    block = pltpu.VMEM((kv_heads, tokens, group, width), bf16)
    hop = pltpu.VMEM((kv_heads, chips) + piece, bf16)
    return pl.pallas_call(
        fused_kernel,
        in_specs=[vmem, vmem, vmem, anywhere, anywhere],
        out_specs=[anywhere, anywhere, vmem, vmem],
        out_shape=[
            jax.ShapeDtypeStruct(queries.shape, bf16),
            jax.ShapeDtypeStruct(queries.shape, bf16),
            jax.ShapeDtypeStruct(keys.shape, bf16),
            jax.ShapeDtypeStruct(keys.shape, bf16),
        ],
        scratch_shapes=[pltpu.VMEM((kv_heads,) + piece, bf16)] + [block] * 4
        + [pltpu.VMEM((kv_heads, 2, chips) + piece, bf16)] * 2
        + [hop] * 5
        + [
            pltpu.VMEM(ids.shape, jnp.int32),
            pltpu.VMEM((length // BLK, rows), f32),
            pltpu.VMEM((length, rows), f32),
            pltpu.VMEM((length, rows), bf16),
        ]
        + [dma((kv_heads,))] * 4
        + [dma((shards,))] * 2
        + [dma((kv_heads, chips))] * 6
        + [dma((kv_heads,))] * 2
        + [dma((kv_heads, chips))] * 4,
        compiler_params=pltpu.CompilerParams(
            collective_id=0, has_side_effects=True, vmem_limit_bytes=60 * 1024 * 1024
        ),
        name="fused",
    )(ids, keys, values, queries, out_grad)


def lane_ids(rand_blocks, global_blocks, shards, here):
    group, block_count, slots = rand_blocks.shape
    ids = rand_blocks.reshape(group, shards, here, slots).transpose(1, 2, 3, 0)
    ids = ids.reshape(shards, here * slots, 1, group)
    reps = 128 // group
    ids = jnp.broadcast_to(ids, (shards, here * slots, reps, group)).reshape(shards, here * slots, 128)
    common = jnp.broadcast_to(global_blocks[None, :, None], (shards, global_blocks.shape[0], 128))
    return jnp.concatenate([ids, common], axis=1)


def body(shards, queries, keys, values, out_grad, rand_blocks, global_blocks):
    tokens, kv_heads, width = keys.shape
    here = tokens // BLK
    block_count = rand_blocks.shape[1]
    group = queries.shape[1] // kv_heads
    me = lax.axis_index("ctx")
    if (shards == kv_heads == group == 8 and here == 2 and rand_blocks.shape[2] == 3
            and global_blocks.shape[0] == 2):
        ids = lane_ids(rand_blocks, global_blocks, shards, here)
        return fused(queries, out_grad, keys, values, ids)
    kv_here = jnp.stack([keys.transpose(1, 0, 2), values.transpose(1, 0, 2)], axis=1)
    kv = lax.all_gather(kv_here, "ctx", axis=0)
    rand_all = lax.all_gather(rand_blocks, "ctx", axis=0, tiled=True)
    bias = row_bias(rand_all, global_blocks, me * here, here, block_count, kv_heads)
    output, query_grad, parts = local_attention(queries, out_grad, kv, bias)
    sums = lax.psum_scatter(parts, "ctx", scatter_dimension=0, tiled=False)
    grads = sums.transpose(1, 2, 0, 3)
    return output, query_grad, grads[0], grads[1]


def solution(mesh):
    split = P(("dp", "ctx"), None, None)
    return jax.shard_map(
        functools.partial(body, mesh.shape["ctx"]),
        mesh=mesh,
        in_specs=(split, split, split, split, split, P("dp")),
        out_specs=(split, split, split, split),
        check_vma=False,
    )
```
